512 devices in a mesh: row: 32 (over z, core), col: 16 (over x, y).
Axes of the slice: x: 4, y: 4, z: 16, core: 2. Of those that a mesh axis runs over, the one named last changes fastest.
Arguments:
- x_points: bfloat16 [131072, 256], P(('row', 'col')), may hold values from -1.5 to 1.5
- y_points: bfloat16 [131072, 256], P(('row', 'col')), may hold values from -1.5 to 1.5
- log_a: float32 [131072], P(('row', 'col')), may hold values from -1.5 to 1.5
- log_b: float32 [131072], P(('row', 'col')), may hold values from -1.5 to 1.5
- g_init: float32 [131072], P(('row', 'col')), may hold values from -3 to 3
- tile_list: int32 [24576, 2], P(('row', 'col')), may hold values from 0 to 1023, as said below
- tile_count: int32 [512], P(('row', 'col')), may hold values from 2 to 48, as said below
Outputs:
- f_out: float32 [131072], P(('row', 'col'))
- g_out: float32 [131072], P(('row', 'col'))
The draws below stay inside these ranges and needn't reach their ends.
Inputs may be any that keep to these rules, and one draw needn't show every extreme that they name: `tile_list`: slots 48 * d to 48 * (d + 1) - 1 belong to device d = row index * 16 + col index. Each slot names a source block held by a device of d's row group and a target block held by a device of d's col group; the slots of one device are distinct pairs. Every block of either cloud is in some active tile. `tile_count`: some device has all 48 slots active.
All inputs are finite; a program needn't handle non-finite values.
Results may differ from the reference program's by a relative error of at most 0.0003.
Values may be sent and summed in bfloat16 or wider, within the bound.
A program may use at most 64 MiB of HBM per device.

```python
import math
import jax
import jax.numpy as jnp
from jax import lax

D = 256
BLOCK = 128
BLK_DEV = 2
TILE_DEV = 48
ITERS = 2
NPTS = 131072
N_ROW = 32
N_COL = 16
DEVICES = 512


def shared_tiles(key):
    local_key = jax.random.fold_in(key, 7301)
    count_key = jax.random.fold_in(key, 7302)
    chosen_key = jax.random.fold_in(key, 7303)
    rows_group = N_COL * BLK_DEV
    cols_group = N_ROW * BLK_DEV
    space = rows_group * cols_group
    device = jnp.arange(DEVICES, dtype=jnp.int32)
    row_of = device // N_COL
    col_of = device % N_COL
    pair = jnp.arange(space, dtype=jnp.int32)
    local_row = pair // cols_group
    local_col = pair % cols_group
    diagonal = (local_row[None, :] // BLK_DEV == col_of[:, None]) & (local_col[None, :] // BLK_DEV == row_of[:, None]) & (local_row % BLK_DEV == local_col % BLK_DEV)[None, :]
    random_bits = jax.random.randint(local_key, (DEVICES, space), 0, 4096, dtype=jnp.int32)
    priority = jnp.where(diagonal, 4096, random_bits) * space + pair[None, :]
    unused, picked = lax.top_k(priority, TILE_DEV)
    picked_row = picked // cols_group
    picked_col = picked % cols_group
    source_block = row_of[:, None] * rows_group + picked_row
    target_block = (picked_col // BLK_DEV * N_COL + col_of[:, None]) * BLK_DEV + picked_col % BLK_DEV
    listing = jnp.stack([source_block, target_block], axis=-1).reshape(DEVICES * TILE_DEV, 2).astype(jnp.int32)
    uniform_int = jax.random.randint(count_key, (DEVICES,), 0, 1025, dtype=jnp.int32)
    counts = BLK_DEV + (TILE_DEV - BLK_DEV) * uniform_int * uniform_int // (1024 * 1024)
    fullest = jax.random.randint(chosen_key, (), 0, DEVICES, dtype=jnp.int32)
    counts = jnp.where(device == fullest, TILE_DEV, counts).astype(jnp.int32)
    return (listing, counts)


def draw_tile_list(key, part):
    return shared_tiles(key)[0]


def draw_tile_count(key, part):
    return shared_tiles(key)[1]


def steps_of(rng, dims, shards, low, top_value):
    factor_of = 1.0
    for dim, blocks in shards:
        draws = jax.random.uniform(jax.random.fold_in(jax.random.fold_in(rng, 6), dim), (blocks,), jnp.float32, low / len(shards), top_value / len(shards))
        factor_of = factor_of * jnp.repeat(jnp.exp(draws), dims[dim] // blocks).reshape((-1,) + (1,) * (len(dims) - 1 - dim))
    return factor_of


def scatter_about(own_key, extent, scale, limit, cuts=(), held_as=jnp.bfloat16):
    entries = scale * jax.random.normal(own_key, extent, jnp.float32)
    if cuts:
        entries = entries * steps_of(own_key, extent, cuts, -0.22, 0.18)
    return jnp.clip(entries, -limit, limit).astype(held_as)


def setup_inputs(seed: int = 0) -> dict:
    keys = jax.random.split(jax.random.key(seed), 8)
    x_points = scatter_about(keys[0], (NPTS, D), 0.25, 1.5, ((0, 512),))
    y_points = scatter_about(keys[1], (NPTS, D), 0.25, 1.5, ((0, 512),))
    log_a = jnp.clip(jax.random.uniform(keys[2], (NPTS,), jnp.float32, -1.5, 1.5) * steps_of(keys[2], (NPTS,), ((0, 512),), -0.4, 0.0), -1.5, 1.5)
    log_b = jnp.clip(jax.random.uniform(keys[3], (NPTS,), jnp.float32, -1.5, 1.5) * steps_of(keys[3], (NPTS,), ((0, 512),), -0.4, 0.0), -1.5, 1.5)
    g_init = scatter_about(keys[4], (NPTS,), 0.5, 3.0, ((0, 512),), jnp.float32)
    tile_list = draw_tile_list(jax.random.fold_in(keys[7], 71), 0)
    tile_count = draw_tile_count(jax.random.fold_in(keys[7], 71), 0)
    return dict(x_points=x_points, y_points=y_points, log_a=log_a, log_b=log_b, g_init=g_init, tile_list=tile_list, tile_count=tile_count)


EPSILON = 0.25
NEGATIVE = -1.0e30


def online_pass(score_of, targets, shape_blocks, turns):
    def visit(carry, turn_index):
        top, total = carry
        scores = score_of(turn_index)
        rows = targets[turn_index]
        new_top = top.at[rows].max(jnp.max(scores, axis=-1))
        total = total * jnp.exp(top - new_top)
        shift = jnp.take(new_top, rows, axis=0)[:, :, None]
        total = total.at[rows].add(jnp.sum(jnp.exp(scores - shift), axis=-1))
        return (new_top, total), None
    start = (jnp.full(shape_blocks, NEGATIVE, jnp.float32), jnp.zeros(shape_blocks, jnp.float32))
    (top, total), unused = lax.scan(visit, start, jnp.arange(turns))
    return -EPSILON * (top + jnp.log(total))


def reference(x_points, y_points, log_a, log_b, g_init, tile_list, tile_count):
    width = x_points.shape[1]
    nblocks = x_points.shape[0] // BLOCK
    x_blocks = x_points.reshape(nblocks, BLOCK, width)
    y_blocks = y_points.reshape(nblocks, BLOCK, width)
    x_square = jnp.sum(jnp.square(x_blocks.astype(jnp.float32)), axis=-1)
    y_square = jnp.sum(jnp.square(y_blocks.astype(jnp.float32)), axis=-1)
    a_blocks = log_a.reshape(nblocks, BLOCK)
    b_blocks = log_b.reshape(nblocks, BLOCK)
    g_blocks = g_init.reshape(nblocks, BLOCK)
    slots = tile_list.shape[0]
    batch = math.gcd(slots, 8)
    turns = slots // batch
    slot_ids = jnp.arange(slots, dtype=jnp.int32)
    active = (slot_ids % TILE_DEV < jnp.take(tile_count, slot_ids // TILE_DEV)).reshape(turns, batch)
    row_ids = tile_list[:, 0].reshape(turns, batch)
    col_ids = tile_list[:, 1].reshape(turns, batch)

    def cost_of(turn_index):
        rows = row_ids[turn_index]
        cols = col_ids[turn_index]
        x_take = jnp.take(x_blocks, rows, axis=0).astype(jnp.float32)
        y_take = jnp.take(y_blocks, cols, axis=0).astype(jnp.float32)
        inner = jnp.einsum("tpd,tqd->tpq", x_take, y_take)
        return 0.5 * jnp.take(x_square, rows, axis=0)[:, :, None] + 0.5 * jnp.take(y_square, cols, axis=0)[:, None, :] - inner

    f_blocks = jnp.zeros_like(a_blocks)
    for iteration in range(ITERS):
        def f_scores(turn_index):
            cols = col_ids[turn_index]
            scores = (jnp.take(g_blocks, cols, axis=0)[:, None, :] - cost_of(turn_index)) / EPSILON + jnp.take(b_blocks, cols, axis=0)[:, None, :]
            return jnp.where(active[turn_index][:, None, None], scores, NEGATIVE)
        f_blocks = online_pass(f_scores, row_ids, a_blocks.shape, turns)

        def g_scores(turn_index):
            rows = row_ids[turn_index]
            scores = (jnp.take(f_blocks, rows, axis=0)[:, :, None] - cost_of(turn_index)) / EPSILON + jnp.take(a_blocks, rows, axis=0)[:, :, None]
            scores = jnp.transpose(scores, (0, 2, 1))
            return jnp.where(active[turn_index][:, None, None], scores, NEGATIVE)
        g_blocks = online_pass(g_scores, col_ids, b_blocks.shape, turns)
    return f_blocks.reshape(-1), g_blocks.reshape(-1)
```

```python
import functools
import math

import jax
import jax.numpy as jnp
from jax import lax
from jax.experimental import pallas as pl
from jax.experimental.pallas import tpu as pltpu
from jax.sharding import PartitionSpec as P

MESH = pl.DeviceIdType.MESH
BLOCK = 128
ITERS = 2
CORES = 2
LOG2E = math.log2(math.e)
LN2 = math.log(2.0)
NEGATIVE = -1e30
TINY = 1e-37
F32 = jnp.float32


def kernel(
    dims,
    tile_ref, count_ref, x_hbm, y_hbm, log_a, log_b, g_init,
    f_out, g_out,
    x_all, y_all, w_all, u_all, kt, kk, tile_top, tile_sum, tile_lse, block_top,
    f_send, f_recv, g_send, g_recv, x_square, y_square,
    in_sem, ring_send, ring_recv, wring_send, wring_recv, mate_sem, xa_send, xa_recv, xb_send, xb_recv,
    f_sem, u_sem, g_sem, w_sem,
):
    nz, nx, ny = dims
    rows, cols = nz * CORES, nx * ny
    tiles = tile_ref.shape[0]
    half = nz // 2
    row, col = lax.axis_index("row"), lax.axis_index("col")
    z, core = row // CORES, row % CORES
    px, py = col // ny, col % ny
    mate = (z * CORES + 1 - core, col)

    def at_z(step):
        return (z + step + nz) % nz * CORES + core

    def at_x(step):
        return (px + step) % nx * ny + py

    def at_y(step):
        return px * ny + (py + step) % ny

    def remote(src, dst, send, recv, device):
        return pltpu.make_async_remote_copy(
            src_ref=src, dst_ref=dst, send_sem=send, recv_sem=recv, device_id=device, device_id_type=MESH
        )

    def drain(ref, sem):
        pltpu.make_async_copy(ref, ref, sem).wait()

    load_x = pltpu.make_async_copy(x_hbm, x_all.at[pl.ds(2 * col, 2)], in_sem.at[0])
    load_y = pltpu.make_async_copy(y_hbm, y_all.at[pl.ds(2 * row, 2)], in_sem.at[1])
    load_y.start()
    load_x.start()

    barrier = pltpu.get_barrier_semaphore()
    greeted = [mate, (at_z(1), col), (at_z(-1), col)]
    greeted += [(row, at_x(k)) for k in range(1, nx)] + [(row, at_y(k)) for k in range(1, ny)]
    for device in greeted:
        pl.semaphore_signal(barrier, inc=1, device_id=device, device_id_type=MESH)
    pl.semaphore_wait(barrier, len(greeted))

    def ring(way, step, part):
        origin = at_z(-(step - 1) if way == 0 else step - 1)
        block = y_all.at[origin * 2 + part]
        return remote(
            block, block, ring_send.at[way, step, part], ring_recv.at[way, step, part],
            (at_z(1 if way == 0 else -1), col),
        )

    def wring(way, step):
        origin = at_z(-(step - 1) if way == 0 else step - 1)
        line = w_all.at[0, origin]
        return remote(
            line, line, wring_send.at[way, step], wring_recv.at[way, step], (at_z(1 if way == 0 else -1), col)
        )

    def to_mate(origin, part):
        block = y_all.at[origin * 2 + part]
        return remote(block, block, mate_sem.at[0], mate_sem.at[1], mate)

    def w_to_mate(origin):
        line = w_all.at[0, origin]
        return remote(line, line, mate_sem.at[2], mate_sem.at[3], mate)

    load_y.wait()
    for part in range(2):
        for way in range(2):
            if half > 1 or part == way:
                ring(way, 1, part).start()
    load_x.wait()
    for k in range(1, nx):
        block = x_all.at[2 * col]
        remote(block, block, xa_send.at[0, k], xa_recv.at[0, k], (row, at_x(k))).start()
    for k in range(1, ny):
        block = x_all.at[2 * col + 1]
        remote(block, block, xa_send.at[1, k], xa_recv.at[1, k], (row, at_y(k))).start()
    for part in range(2):
        to_mate(row, part).start()

    diagonal = lax.broadcasted_iota(jnp.int32, (BLOCK, BLOCK), 0) == lax.broadcasted_iota(
        jnp.int32, (BLOCK, BLOCK), 1
    )

    def squares(block):
        value = block.astype(F32)
        total = jnp.sum(value * value, axis=1, keepdims=True)
        return jnp.sum(jnp.where(diagonal, total, 0.0), axis=0, keepdims=True)

    for part in range(2):
        y_square[part : part + 1, :] = squares(y_all[2 * row + part])
    w_all[0, row] = LOG2E * (4.0 * g_init[...] - 2.0 * y_square[...] + log_b[...])
    wring(0, 1).start()
    if half > 1:
        wring(1, 1).start()
    w_to_mate(row).start()
    for part in range(2):
        x_square[part : part + 1, :] = squares(x_all[2 * col + part])

    def send_plane():
        for k in range(nx):
            if k:
                block = x_all.at[2 * at_x(nx - k)]
                remote(block, block, xa_send.at[0, k], xa_recv.at[0, k], (row, col)).wait_recv()
            block = x_all.at[2 * at_x(nx - k)]
            for j in range(1, ny):
                remote(block, block, xb_send.at[0], xb_recv.at[0], (row, at_y(j))).start()
        for k in range(ny):
            if k:
                block = x_all.at[2 * at_y(ny - k) + 1]
                remote(block, block, xa_send.at[1, k], xa_recv.at[1, k], (row, col)).wait_recv()
            block = x_all.at[2 * at_y(ny - k) + 1]
            for j in range(1, nx):
                remote(block, block, xb_send.at[1], xb_recv.at[1], (row, at_x(j))).start()

    for step in range(1, half + 1):
        last, before_last = step == half, step == half - 1
        for part in range(2):
            for way in range(2):
                if last and part != way:
                    continue
                origin = at_z(-step if way == 0 else step)
                ring(way, step, part).wait_recv()
                if not last and not (before_last and part != way):
                    ring(way, step + 1, part).start()
                to_mate(origin, part).start()
                if part == 1 and not last:
                    wring(way, step).wait_recv()
                    if not (before_last and way == 1):
                        wring(way, step + 1).start()
                    w_to_mate(origin).start()
        if last:
            wring(0, step).wait_recv()
            w_to_mate(at_z(-step)).start()
        if step == min(2, half):
            send_plane()

    for lane, (outer, inner) in enumerate(((nx, ny), (ny, nx))):
        if inner > 1:
            drain(x_all.at[pl.ds(0, outer * (inner - 1))], xb_recv.at[lane])
    drain(y_all.at[pl.ds(0, rows)], mate_sem.at[1])
    drain(w_all.at[0, pl.ds(0, nz)], mate_sem.at[3])

    def row_id(t):
        return tile_ref[t, 0] % (2 * cols)

    def col_id(t):
        block = tile_ref[t, 1]
        return block // (2 * cols) * 2 + block % 2

    def column_of(line):
        return jnp.transpose(jnp.broadcast_to(line, (BLOCK, BLOCK)))

    def reduce_tile(t, scores):
        top = jnp.max(scores, axis=0, keepdims=True)
        tile_top[pl.ds(t, 1), :] = top
        tile_sum[pl.ds(t, 1), :] = jnp.sum(jnp.exp2(scores - top), axis=0, keepdims=True)

    def product(left, right):
        return lax.dot_general(left, right, (((1,), (1,)), ((), ())), preferred_element_type=F32) * (4.0 * LOG2E)

    def loop(body, unroll):
        def step(t, carry):
            body(t)
            return carry

        lax.fori_loop(0, tiles, step, 0, unroll=unroll)

    def combine(id_of, blocks):
        alive = lax.broadcasted_iota(jnp.int32, (tiles, BLOCK), 0) < count_ref[0]
        tile_lse[...] = jnp.where(alive, tile_top[...] + jnp.log2(tile_sum[...]), NEGATIVE)
        place = lax.broadcasted_iota(jnp.int32, (blocks, BLOCK), 0)

        def top_of(t, top):
            return jnp.maximum(top, jnp.where(place == id_of(t), tile_lse[pl.ds(t, 1), :], NEGATIVE))

        top = lax.fori_loop(0, tiles, top_of, jnp.full((blocks, BLOCK), NEGATIVE, F32), unroll=4)
        block_top[pl.ds(0, blocks), :] = top

        def sum_of(t, total):
            home = id_of(t)
            share = jnp.exp2(tile_lse[pl.ds(t, 1), :] - block_top[pl.ds(home, 1), :])
            return total + jnp.where(place == home, share, 0.0)

        total = lax.fori_loop(0, tiles, sum_of, jnp.zeros((blocks, BLOCK), F32), unroll=4)
        return top + jnp.log2(jnp.maximum(total, TINY))

    def merge(parts):
        top = jnp.max(parts, axis=0)
        return top + jnp.log2(jnp.sum(jnp.exp2(parts - top[None]), axis=0))

    def spread(value, out):
        for k in range(value.shape[0] // 2):
            out[k] = value[2 * k : 2 * k + 2, :]

    def each(count, body):
        def step(k, carry):
            body(k)
            return carry

        lax.fori_loop(1, count, step, 0)

    for it in range(ITERS):
        def f_tile(t):
            line, part = col_id(t) // 2, col_id(t) % 2
            if it == 0:
                kt[t] = product(y_all[col_id(t)], x_all[row_id(t)])
            reduce_tile(t, kt[t] + column_of(w_all[it, line, pl.ds(part, 1), :]))

        loop(f_tile, 2)
        spread(combine(row_id, cols * 2), f_send.at[it])

        def send_f(k):
            owner = (col + k) % cols
            remote(
                f_send.at[it, owner], f_recv.at[it, col], f_sem.at[it, 0], f_sem.at[it, 1], (row, owner)
            ).start()

        each(cols, send_f)
        f_recv[it, col] = f_send[it, col]
        if it == 0:

            def other(t):
                kk[t] = product(x_all[row_id(t)], y_all[col_id(t)])

            loop(other, 2)
        drain(f_recv.at[it, pl.ds(0, cols - 1)], f_sem.at[it, 1])
        lse = merge(f_recv[it])
        u_all[it, col] = LOG2E * log_a[...] - lse

        def send_u(k):
            line = u_all.at[it, col]
            remote(line, line, u_sem.at[it, 0], u_sem.at[it, 1], (row, (col + k) % cols)).start()

        each(cols, send_u)
        if it == ITERS - 1:
            f_out[...] = 0.5 * x_square[...] - (0.25 * LN2) * lse
        drain(u_all.at[it, pl.ds(0, cols - 1)], u_sem.at[it, 1])

        def g_tile(t):
            line, part = row_id(t) // 2, row_id(t) % 2
            reduce_tile(t, kk[t] + column_of(u_all[it, line, pl.ds(part, 1), :]))

        loop(g_tile, 2)
        spread(combine(col_id, rows * 2), g_send.at[it])

        def send_g(k):
            owner = (row + k) % rows
            remote(
                g_send.at[it, owner], g_recv.at[it, row], g_sem.at[it, 0], g_sem.at[it, 1], (owner, col)
            ).start()

        each(rows, send_g)
        g_recv[it, row] = g_send[it, row]
        drain(g_recv.at[it, pl.ds(0, rows - 1)], g_sem.at[it, 1])
        lse = merge(g_recv[it])
        if it == ITERS - 1:
            g_out[...] = 0.5 * y_square[...] - (0.25 * LN2) * lse
        else:
            w_all[it + 1, row] = LOG2E * log_b[...] - lse

            def send_w(k):
                line = w_all.at[it + 1, row]
                remote(line, line, w_sem.at[it, 0], w_sem.at[it, 1], ((row + k) % rows, col)).start()

            each(rows, send_w)
            drain(w_all.at[it + 1, pl.ds(0, rows - 1)], w_sem.at[it, 1])

    for part in range(2):
        for way in range(2):
            for step in range(1, half + 1):
                if not (step == half and part != way):
                    ring(way, step, part).wait_send()
    for step in range(1, half + 1):
        wring(0, step).wait_send()
        if step < half:
            wring(1, step).wait_send()
    drain(y_all.at[pl.ds(0, rows)], mate_sem.at[0])
    drain(w_all.at[0, pl.ds(0, nz)], mate_sem.at[2])
    for lane, (outer, inner) in enumerate(((nx, ny), (ny, nx))):
        for k in range(1, outer):
            block = x_all.at[0]
            remote(block, block, xa_send.at[lane, k], xa_recv.at[lane, k], (row, at_x(1))).wait_send()
        if inner > 1:
            drain(x_all.at[pl.ds(0, outer * (inner - 1))], xb_send.at[lane])
    for it in range(ITERS):
        drain(f_recv.at[it, pl.ds(0, cols - 1)], f_sem.at[it, 0])
        drain(u_all.at[it, pl.ds(0, cols - 1)], u_sem.at[it, 0])
        drain(g_recv.at[it, pl.ds(0, rows - 1)], g_sem.at[it, 0])
        if it < ITERS - 1:
            drain(w_all.at[it + 1, pl.ds(0, rows - 1)], w_sem.at[it, 0])


def body(dims, x_points, y_points, log_a, log_b, g_init, tile_list, tile_count):
    nz, nx, ny = dims
    rows, cols = nz * CORES, nx * ny
    width = x_points.shape[1]
    tiles = tile_list.shape[0]
    half = nz // 2
    vmem = pl.BlockSpec(memory_space=pltpu.VMEM)
    smem = pl.BlockSpec(memory_space=pltpu.SMEM)
    anywhere = pl.BlockSpec(memory_space=pl.ANY)
    dma = pltpu.SemaphoreType.DMA
    line = jax.ShapeDtypeStruct((2, BLOCK), F32)
    f_out, g_out = pl.pallas_call(
        functools.partial(kernel, dims),
        out_shape=(line, line),
        in_specs=[smem, smem, anywhere, anywhere, vmem, vmem, vmem],
        out_specs=(vmem, vmem),
        scratch_shapes=[
            pltpu.VMEM((cols * 2, BLOCK, width), jnp.bfloat16),
            pltpu.VMEM((rows * 2, BLOCK, width), jnp.bfloat16),
            pltpu.VMEM((ITERS, rows, 2, BLOCK), F32),
            pltpu.VMEM((ITERS, cols, 2, BLOCK), F32),
            pltpu.VMEM((tiles, BLOCK, BLOCK), F32),
            pltpu.VMEM((tiles, BLOCK, BLOCK), F32),
            pltpu.VMEM((tiles, BLOCK), F32),
            pltpu.VMEM((tiles, BLOCK), F32),
            pltpu.VMEM((tiles, BLOCK), F32),
            pltpu.VMEM((max(rows, cols) * 2, BLOCK), F32),
            pltpu.VMEM((ITERS, cols, 2, BLOCK), F32),
            pltpu.VMEM((ITERS, cols, 2, BLOCK), F32),
            pltpu.VMEM((ITERS, rows, 2, BLOCK), F32),
            pltpu.VMEM((ITERS, rows, 2, BLOCK), F32),
            pltpu.VMEM((2, BLOCK), F32),
            pltpu.VMEM((2, BLOCK), F32),
            dma((2,)),
            dma((2, half + 1, 2)),
            dma((2, half + 1, 2)),
            dma((2, half + 1)),
            dma((2, half + 1)),
            dma((4,)),
            dma((2, max(nx, ny))),
            dma((2, max(nx, ny))),
            dma((2,)),
            dma((2,)),
            dma((ITERS, 2)),
            dma((ITERS, 2)),
            dma((ITERS, 2)),
            dma((ITERS, 2)),
        ],
        compiler_params=pltpu.CompilerParams(collective_id=0, has_side_effects=True),
    )(
        tile_list,
        tile_count,
        x_points.reshape(2, BLOCK, width),
        y_points.reshape(2, BLOCK, width),
        log_a.reshape(2, BLOCK),
        log_b.reshape(2, BLOCK),
        g_init.reshape(2, BLOCK),
    )
    return f_out.reshape(-1), g_out.reshape(-1)


def solution(mesh):
    rows, cols = mesh.shape["row"], mesh.shape["col"]
    side = math.isqrt(cols)
    dims = (rows // CORES, cols // side, side)
    whole = P(("row", "col"))
    grid = P(("row", "col"), None)
    return jax.shard_map(
        functools.partial(body, dims),
        mesh=mesh,
        in_specs=(grid, grid, whole, whole, whole, grid, whole),
        out_specs=(whole, whole),
        check_vma=False,
    )
```

```python
import functools
import math

import jax
import jax.numpy as jnp
from jax import lax
from jax.experimental import pallas as pl
from jax.experimental.pallas import tpu as pltpu
from jax.sharding import PartitionSpec as P

MESH = pl.DeviceIdType.MESH
BLOCK = 128
ITERS = 2
CORES = 2
LOG2E = math.log2(math.e)
LN2 = math.log(2.0)
NEGATIVE = -1e30
TINY = 1e-37
F32 = jnp.float32
PIECES = 4
UNROLL = 8


def kernel(
    dims,
    tile_ref, count_ref, x_hbm, y_hbm, log_a, log_b, g_init,
    f_out, g_out,
    x_all, y_all, w_all, u_all, kt, kk, tile_top, tile_sum, tile_lse, block_top,
    f_send, f_recv, g_send, g_recv, x_square, y_square,
    in_sem, ring_send, ring_recv, wring_send, wring_recv, mate_sem, xa_send, xa_recv,
    f_sem, u_sem, g_sem, w_sem,
):
    nz, nx, ny = dims
    rows, cols = nz * CORES, nx * ny
    tiles = tile_ref.shape[1]
    half = nz // 2
    row, col = lax.axis_index("row"), lax.axis_index("col")
    z, core = row // CORES, row % CORES
    px, py = col // ny, col % ny
    mate = (z * CORES + 1 - core, col)

    def at_z(step):
        return (z + step + nz) % nz * CORES + core

    def at_x(step):
        return (px + step) % nx * ny + py

    def at_y(step):
        return px * ny + (py + step) % ny

    def remote(src, dst, send, recv, device):
        return pltpu.make_async_remote_copy(
            src_ref=src, dst_ref=dst, send_sem=send, recv_sem=recv, device_id=device, device_id_type=MESH
        )

    def drain(ref, sem):
        pltpu.make_async_copy(ref, ref, sem).wait()

    pending = []

    def later(wait, *args):
        pending.append(lambda: wait(*args))

    load_x = pltpu.make_async_copy(x_hbm, x_all.at[pl.ds(2 * col, 2)], in_sem.at[0])
    load_y = pltpu.make_async_copy(y_hbm, y_all.at[pl.ds(2 * row, 2)], in_sem.at[1])
    load_y.start()
    load_x.start()

    barrier = pltpu.get_barrier_semaphore()
    greeted = [mate, (at_z(1), col), (at_z(-1), col)]
    greeted += [(row, at_x(1)), (row, at_x(nx - 1)), (row, at_y(1)), (row, at_y(ny - 1))]
    for device in greeted:
        pl.semaphore_signal(barrier, inc=1, device_id=device, device_id_type=MESH)
    pl.semaphore_wait(barrier, len(greeted))


    size = 2 * BLOCK // PIECES

    def piece(origin, part):
        return y_all.at[origin * 2 + part * size // BLOCK, pl.ds(part * size % BLOCK, size)]

    def ring(way, step, part):
        block = piece(at_z(-(step - 1) if way == 0 else step - 1), part)
        return remote(
            block, block, ring_send.at[way, step, part], ring_recv.at[way, step, part],
            (at_z(1 if way == 0 else -1), col),
        )

    def wring(way, step):
        origin = at_z(-(step - 1) if way == 0 else step - 1)
        line = w_all.at[0, origin]
        return remote(
            line, line, wring_send.at[way, step], wring_recv.at[way, step], (at_z(1 if way == 0 else -1), col)
        )

    def to_mate(origin, part):
        block = piece(origin, part)
        return remote(block, block, mate_sem.at[0], mate_sem.at[1], mate)

    def w_to_mate(origin):
        line = w_all.at[0, origin]
        return remote(line, line, mate_sem.at[2], mate_sem.at[3], mate)

    def go(copy):
        copy.start()
        later(copy.wait_send)

    def travels(way, step, part):
        return 1 <= step < half or (step == half and (part < PIECES // 2) == (way == 0))

    def at_line(axis, step):
        return at_x(step) if axis == 0 else at_y(step)

    def at_both(axis, one, two):
        x, y = (one, two) if axis == 0 else (two, one)
        return (px + x + nx) % nx * ny + (py + y + ny) % ny

    def plane(lane, phase, way, hop, index):
        axis = lane if phase == 0 else 1 - lane
        sign = 1 if way == 0 else -1
        back = 0 if hop == 0 else -sign
        origin = at_both(lane, back, 0) if phase == 0 else at_both(lane, index, back)
        block = x_all.at[2 * origin + lane]
        if hop == 1:
            block = block.at[pl.ds(way * (BLOCK // 2), BLOCK // 2)]
        sems = (lane, phase, way, hop, index)
        return remote(block, block, xa_send.at[sems], xa_recv.at[sems], (row, at_line(axis, sign)))

    load_y.wait()
    for part in range(PIECES):
        for way in range(2):
            if travels(way, 1, part):
                go(ring(way, 1, part))
    load_x.wait()
    for lane in range(2):
        for way in range(2):
            go(plane(lane, 0, way, 0, 0))
    for lane in range(2):
        for way in range(2):
            go(plane(lane, 1, way, 0, 0))
    for part in range(PIECES):
        to_mate(row, part).start()

    diagonal = lax.broadcasted_iota(jnp.int32, (BLOCK, BLOCK), 0) == lax.broadcasted_iota(
        jnp.int32, (BLOCK, BLOCK), 1
    )

    def squares(block):
        value = block.astype(F32)
        total = jnp.sum(value * value, axis=1, keepdims=True)
        return jnp.sum(jnp.where(diagonal, total, 0.0), axis=0, keepdims=True)

    for part in range(2):
        y_square[part : part + 1, :] = squares(y_all[2 * row + part])
    w_all[0, row] = LOG2E * (4.0 * g_init[...] - 2.0 * y_square[...] + log_b[...])
    go(wring(0, 1))
    go(wring(1, 1))
    w_to_mate(row).start()
    for part in range(2):
        x_square[part : part + 1, :] = squares(x_all[2 * col + part])

    def plane_steps(stage):
        for lane in range(2):
            if stage == 1:
                for way in range(2):
                    plane(lane, 0, way, 0, 0).wait_recv()
                    go(plane(lane, 0, way, 1, 0))
                    for out in range(2):
                        go(plane(lane, 1, out, 0, 3 if way == 0 else 1))
            if stage == 2:
                for way in range(2):
                    plane(lane, 0, way, 1, 0).wait_recv()
                for out in range(2):
                    go(plane(lane, 1, out, 0, 2))
            if stage in (1, 2, 3, 4):
                index = (0, 0, 1, 3, 2)[stage]
                for way in range(2):
                    plane(lane, 1, way, 0, index).wait_recv()
                    go(plane(lane, 1, way, 1, index))
            if stage == 5:
                for index in range(4):
                    for way in range(2):
                        plane(lane, 1, way, 1, index).wait_recv()

    def pass_lines(step):
        for way in range(2):
            if 1 <= step < half or (step == half and way == 0):
                wring(way, step).wait_recv()
                if step + 1 < half or (step + 1 == half and way == 0):
                    go(wring(way, step + 1))
                w_to_mate(at_z(-step if way == 0 else step)).start()

    for step in range(1, max(half, 5) + 1):
        for part in range(PIECES):
            for way in range(2):
                if not travels(way, step, part):
                    continue
                ring(way, step, part).wait_recv()
                if travels(way, step + 1, part):
                    go(ring(way, step + 1, part))
                to_mate(at_z(-step if way == 0 else step), part).start()
            if part == 0 and step <= half:
                pass_lines(step - 1)
        plane_steps(step)
    pass_lines(half)
    drain(y_all.at[pl.ds(0, rows)], mate_sem.at[1])
    later(drain, y_all.at[pl.ds(0, rows)], mate_sem.at[0])
    drain(w_all.at[0, pl.ds(0, nz)], mate_sem.at[3])
    later(drain, w_all.at[0, pl.ds(0, nz)], mate_sem.at[2])

    def row_id(t):
        return tile_ref[0, t] % (2 * cols)

    def col_id(t):
        block = tile_ref[1, t]
        return block // (2 * cols) * 2 + block % 2

    def column_of(line):
        return jnp.sum(jnp.where(diagonal, line, 0.0), axis=1, keepdims=True)

    def reduce_tile(t, scores):
        top = jnp.max(scores, axis=0, keepdims=True)
        tile_top[pl.ds(t, 1), :] = top
        tile_sum[pl.ds(t, 1), :] = jnp.sum(jnp.exp2(scores - top), axis=0, keepdims=True)

    def product(left, right):
        return lax.dot_general(left, right, (((1,), (1,)), ((), ())), preferred_element_type=F32) * (4.0 * LOG2E)

    def loop(body, unroll):
        def step(t, carry):
            body(t)
            return carry

        lax.fori_loop(0, tiles, step, 0, unroll=unroll)

    def combine(id_of, blocks):
        alive = lax.broadcasted_iota(jnp.int32, (tiles, BLOCK), 0) < count_ref[0]
        tile_lse[...] = jnp.where(alive, tile_top[...] + jnp.log2(tile_sum[...]), NEGATIVE)
        place = lax.broadcasted_iota(jnp.int32, (blocks, BLOCK), 0)

        def top_of(t, top):
            return jnp.maximum(top, jnp.where(place == id_of(t), tile_lse[pl.ds(t, 1), :], NEGATIVE))

        top = lax.fori_loop(0, tiles, top_of, jnp.full((blocks, BLOCK), NEGATIVE, F32), unroll=4)
        block_top[pl.ds(0, blocks), :] = top

        def sum_of(t, total):
            home = id_of(t)
            share = jnp.exp2(tile_lse[pl.ds(t, 1), :] - block_top[pl.ds(home, 1), :])
            return total + jnp.where(place == home, share, 0.0)

        total = lax.fori_loop(0, tiles, sum_of, jnp.zeros((blocks, BLOCK), F32), unroll=4)
        return top + jnp.log2(jnp.maximum(total, TINY))

    def merge(parts):
        top = jnp.max(parts, axis=0)
        return top + jnp.log2(jnp.sum(jnp.exp2(parts - top[None]), axis=0))

    def spread(value, out):
        for k in range(value.shape[0] // 2):
            out[k] = value[2 * k : 2 * k + 2, :]

    def each(count, body):
        def step(k, carry):
            body(count // 2 + k // 2 * (1 - k % 2 * 2))
            return carry

        lax.fori_loop(1, count, step, 0)

    for it in range(ITERS):
        def f_tile(t):
            line, part = col_id(t) // 2, col_id(t) % 2
            if it == 0:
                kt[t] = product(y_all[col_id(t)], x_all[row_id(t)])
            reduce_tile(t, kt[t] + column_of(w_all[it, line, pl.ds(part, 1), :]))

        loop(f_tile, UNROLL)
        spread(combine(row_id, cols * 2), f_send.at[it])

        def send_f(k):
            owner = (col + k) % cols
            remote(
                f_send.at[it, owner], f_recv.at[it, col], f_sem.at[it, 0], f_sem.at[it, 1], (row, owner)
            ).start()

        each(cols, send_f)
        later(drain, f_recv.at[it, pl.ds(0, cols - 1)], f_sem.at[it, 0])
        f_recv[it, col] = f_send[it, col]
        if it == 0:

            def other(t):
                kk[t] = product(x_all[row_id(t)], y_all[col_id(t)])

            loop(other, 4)
        drain(f_recv.at[it, pl.ds(0, cols - 1)], f_sem.at[it, 1])
        lse = merge(f_recv[it])
        u_all[it, col] = LOG2E * log_a[...] - lse

        def send_u(k):
            line = u_all.at[it, col]
            remote(line, line, u_sem.at[it, 0], u_sem.at[it, 1], (row, (col + k) % cols)).start()

        each(cols, send_u)
        later(drain, u_all.at[it, pl.ds(0, cols - 1)], u_sem.at[it, 0])
        if it == ITERS - 1:
            f_out[...] = 0.5 * x_square[...] - (0.25 * LN2) * lse
        drain(u_all.at[it, pl.ds(0, cols - 1)], u_sem.at[it, 1])

        def g_tile(t):
            line, part = row_id(t) // 2, row_id(t) % 2
            reduce_tile(t, kk[t] + column_of(u_all[it, line, pl.ds(part, 1), :]))

        loop(g_tile, UNROLL)
        spread(combine(col_id, rows * 2), g_send.at[it])

        def send_g(k):
            owner = (row + k) % rows
            remote(
                g_send.at[it, owner], g_recv.at[it, row], g_sem.at[it, 0], g_sem.at[it, 1], (owner, col)
            ).start()

        each(rows, send_g)
        later(drain, g_recv.at[it, pl.ds(0, rows - 1)], g_sem.at[it, 0])
        g_recv[it, row] = g_send[it, row]
        drain(g_recv.at[it, pl.ds(0, rows - 1)], g_sem.at[it, 1])
        lse = merge(g_recv[it])
        if it == ITERS - 1:
            g_out[...] = 0.5 * y_square[...] - (0.25 * LN2) * lse
        else:
            w_all[it + 1, row] = LOG2E * log_b[...] - lse

            def send_w(k):
                line = w_all.at[it + 1, row]
                remote(line, line, w_sem.at[it, 0], w_sem.at[it, 1], ((row + k) % rows, col)).start()

            each(rows, send_w)
            later(drain, w_all.at[it + 1, pl.ds(0, rows - 1)], w_sem.at[it, 0])
            drain(w_all.at[it + 1, pl.ds(0, rows - 1)], w_sem.at[it, 1])

    for wait in pending:
        wait()


def body(dims, x_points, y_points, log_a, log_b, g_init, tile_list, tile_count):
    nz, nx, ny = dims
    rows, cols = nz * CORES, nx * ny
    width = x_points.shape[1]
    tiles = tile_list.shape[0]
    half = nz // 2
    vmem = pl.BlockSpec(memory_space=pltpu.VMEM)
    smem = pl.BlockSpec(memory_space=pltpu.SMEM)
    anywhere = pl.BlockSpec(memory_space=pl.ANY)
    dma = pltpu.SemaphoreType.DMA
    line = jax.ShapeDtypeStruct((2, BLOCK), F32)
    f_out, g_out = pl.pallas_call(
        functools.partial(kernel, dims),
        out_shape=(line, line),
        in_specs=[smem, smem, anywhere, anywhere, vmem, vmem, vmem],
        out_specs=(vmem, vmem),
        scratch_shapes=[
            pltpu.VMEM((cols * 2, BLOCK, width), jnp.bfloat16),
            pltpu.VMEM((rows * 2, BLOCK, width), jnp.bfloat16),
            pltpu.VMEM((ITERS, rows, 2, BLOCK), F32),
            pltpu.VMEM((ITERS, cols, 2, BLOCK), F32),
            pltpu.VMEM((tiles, BLOCK, BLOCK), F32),
            pltpu.VMEM((tiles, BLOCK, BLOCK), F32),
            pltpu.VMEM((tiles, BLOCK), F32),
            pltpu.VMEM((tiles, BLOCK), F32),
            pltpu.VMEM((tiles, BLOCK), F32),
            pltpu.VMEM((max(rows, cols) * 2, BLOCK), F32),
            pltpu.VMEM((ITERS, cols, 2, BLOCK), F32),
            pltpu.VMEM((ITERS, cols, 2, BLOCK), F32),
            pltpu.VMEM((ITERS, rows, 2, BLOCK), F32),
            pltpu.VMEM((ITERS, rows, 2, BLOCK), F32),
            pltpu.VMEM((2, BLOCK), F32),
            pltpu.VMEM((2, BLOCK), F32),
            dma((2,)),
            dma((2, half + 1, PIECES)),
            dma((2, half + 1, PIECES)),
            dma((2, half + 1)),
            dma((2, half + 1)),
            dma((4,)),
            dma((2, 2, 2, 2, 4)),
            dma((2, 2, 2, 2, 4)),
            dma((ITERS, 2)),
            dma((ITERS, 2)),
            dma((ITERS, 2)),
            dma((ITERS, 2)),
        ],
        compiler_params=pltpu.CompilerParams(collective_id=0, has_side_effects=True),
    )(
        tile_list.T,
        tile_count,
        x_points.reshape(2, BLOCK, width),
        y_points.reshape(2, BLOCK, width),
        log_a.reshape(2, BLOCK),
        log_b.reshape(2, BLOCK),
        g_init.reshape(2, BLOCK),
    )
    return f_out.reshape(-1), g_out.reshape(-1)


def solution(mesh):
    rows, cols = mesh.shape["row"], mesh.shape["col"]
    side = math.isqrt(cols)
    dims = (rows // CORES, cols // side, side)
    whole = P(("row", "col"))
    grid = P(("row", "col"), None)
    return jax.shard_map(
        functools.partial(body, dims),
        mesh=mesh,
        in_specs=(grid, grid, whole, whole, whole, grid, whole),
        out_specs=(whole, whole),
        check_vma=False,
    )
```

```python
import functools
import math

import jax
import jax.numpy as jnp
from jax import lax
from jax.experimental import pallas as pl
from jax.experimental.pallas import tpu as pltpu
from jax.sharding import PartitionSpec as P

MESH = pl.DeviceIdType.MESH
BLOCK = 128
ITERS = 2
CORES = 2
LOG2E = math.log2(math.e)
LN2 = math.log(2.0)
NEGATIVE = -1e30
TINY = 1e-37
F32 = jnp.float32
PIECES = 4
UNROLL = 8


def kernel(
    dims,
    tile_ref, count_ref, x_hbm, y_hbm, log_a, log_b, g_init,
    f_out, g_out,
    x_all, y_all, w_all, u_all, a_all, a_rows, kt, kk, tile_top, tile_sum, tile_lse, block_top,
    f_send, f_recv, g_send, g_recv, x_square, y_square,
    in_sem, ring_send, ring_recv, wring_send, wring_recv, mate_sem, xa_send, xa_recv,
    f_sem, u_sem, g_sem, w_sem,
):
    nz, nx, ny = dims
    rows, cols = nz * CORES, nx * ny
    tiles = tile_ref.shape[1]
    half = nz // 2
    row, col = lax.axis_index("row"), lax.axis_index("col")
    z, core = row // CORES, row % CORES
    px, py = col // ny, col % ny
    mate = (z * CORES + 1 - core, col)

    def at_z(step):
        return (z + step + nz) % nz * CORES + core

    def at_x(step):
        return (px + step) % nx * ny + py

    def at_y(step):
        return px * ny + (py + step) % ny

    def remote(src, dst, send, recv, device):
        return pltpu.make_async_remote_copy(
            src_ref=src, dst_ref=dst, send_sem=send, recv_sem=recv, device_id=device, device_id_type=MESH
        )

    def drain(ref, sem):
        pltpu.make_async_copy(ref, ref, sem).wait()

    pending = []

    def later(wait, *args):
        pending.append(lambda: wait(*args))

    load_x = pltpu.make_async_copy(x_hbm, x_all.at[pl.ds(2 * col, 2)], in_sem.at[0])
    load_y = pltpu.make_async_copy(y_hbm, y_all.at[pl.ds(2 * row, 2)], in_sem.at[1])
    load_y.start()
    load_x.start()

    barrier = pltpu.get_barrier_semaphore()
    greeted = [mate, (at_z(1), col), (at_z(-1), col)]
    greeted += [(row, at_x(1)), (row, at_x(nx - 1)), (row, at_y(1)), (row, at_y(ny - 1))]
    for device in greeted:
        pl.semaphore_signal(barrier, inc=1, device_id=device, device_id_type=MESH)
    pl.semaphore_wait(barrier, len(greeted))


    size = 2 * BLOCK // PIECES

    def piece(origin, part):
        return y_all.at[origin * 2 + part * size // BLOCK, pl.ds(part * size % BLOCK, size)]

    def ring(way, step, part):
        block = piece(at_z(-(step - 1) if way == 0 else step - 1), part)
        return remote(
            block, block, ring_send.at[way, step, part], ring_recv.at[way, step, part],
            (at_z(1 if way == 0 else -1), col),
        )

    def wring(way, step):
        origin = at_z(-(step - 1) if way == 0 else step - 1)
        line = w_all.at[0, origin]
        return remote(
            line, line, wring_send.at[way, step], wring_recv.at[way, step], (at_z(1 if way == 0 else -1), col)
        )

    def to_mate(origin, part):
        block = piece(origin, part)
        return remote(block, block, mate_sem.at[0], mate_sem.at[1], mate)

    def w_to_mate(origin):
        line = w_all.at[0, origin]
        return remote(line, line, mate_sem.at[2], mate_sem.at[3], mate)

    def go(copy):
        copy.start()
        later(copy.wait_send)

    def travels(way, step, part):
        return 1 <= step < half or (step == half and (part < PIECES // 2) == (way == 0))

    def at_line(axis, step):
        return at_x(step) if axis == 0 else at_y(step)

    def at_both(axis, one, two):
        x, y = (one, two) if axis == 0 else (two, one)
        return (px + x + nx) % nx * ny + (py + y + ny) % ny

    def plane(lane, phase, way, hop, index):
        axis = lane if phase == 0 else 1 - lane
        sign = 1 if way == 0 else -1
        back = 0 if hop == 0 else -sign
        origin = at_both(lane, back, 0) if phase == 0 else at_both(lane, index, back)
        block = x_all.at[2 * origin + lane]
        if hop == 1:
            block = block.at[pl.ds(way * (BLOCK // 2), BLOCK // 2)]
        sems = (lane, phase, way, hop, index)
        return remote(block, block, xa_send.at[sems], xa_recv.at[sems], (row, at_line(axis, sign)))

    load_y.wait()
    for part in range(PIECES):
        for way in range(2):
            if travels(way, 1, part):
                go(ring(way, 1, part))
    load_x.wait()
    for lane in range(2):
        for way in range(2):
            go(plane(lane, 0, way, 0, 0))
    for lane in range(2):
        for way in range(2):
            go(plane(lane, 1, way, 0, 0))
    for part in range(PIECES):
        to_mate(row, part).start()

    diagonal = lax.broadcasted_iota(jnp.int32, (BLOCK, BLOCK), 0) == lax.broadcasted_iota(
        jnp.int32, (BLOCK, BLOCK), 1
    )

    def squares(block):
        value = block.astype(F32)
        total = jnp.sum(value * value, axis=1, keepdims=True)
        return jnp.sum(jnp.where(diagonal, total, 0.0), axis=0, keepdims=True)

    for part in range(2):
        y_square[part : part + 1, :] = squares(y_all[2 * row + part])
    w_all[0, row] = LOG2E * (4.0 * g_init[...] - 2.0 * y_square[...] + log_b[...])
    go(wring(0, 1))
    if half > 1:
        go(wring(1, 1))
    w_to_mate(row).start()
    for part in range(2):
        x_square[part : part + 1, :] = squares(x_all[2 * col + part])

    def plane_steps(stage):
        for lane in range(2):
            if stage == 1:
                for way in range(2):
                    plane(lane, 0, way, 0, 0).wait_recv()
                    go(plane(lane, 0, way, 1, 0))
                    for out in range(2):
                        go(plane(lane, 1, out, 0, 3 if way == 0 else 1))
            if stage == 2:
                for way in range(2):
                    plane(lane, 0, way, 1, 0).wait_recv()
                for out in range(2):
                    go(plane(lane, 1, out, 0, 2))
            if stage in (1, 2, 3, 4):
                index = (0, 0, 1, 3, 2)[stage]
                for way in range(2):
                    plane(lane, 1, way, 0, index).wait_recv()
                    go(plane(lane, 1, way, 1, index))
            if stage == 5:
                for index in range(4):
                    for way in range(2):
                        plane(lane, 1, way, 1, index).wait_recv()

    def pass_lines(step):
        for way in range(2):
            if 1 <= step < half or (step == half and way == 0):
                wring(way, step).wait_recv()
                if step + 1 < half or (step + 1 == half and way == 0):
                    go(wring(way, step + 1))
                w_to_mate(at_z(-step if way == 0 else step)).start()

    for step in range(1, max(half, 5) + 1):
        for part in range(PIECES):
            for way in range(2):
                if not travels(way, step, part):
                    continue
                ring(way, step, part).wait_recv()
                if travels(way, step + 1, part):
                    go(ring(way, step + 1, part))
                to_mate(at_z(-step if way == 0 else step), part).start()
            if part == 0 and step <= half:
                pass_lines(step - 1)
        plane_steps(step)
    pass_lines(half)
    drain(y_all.at[pl.ds(0, rows)], mate_sem.at[1])
    later(drain, y_all.at[pl.ds(0, rows)], mate_sem.at[0])
    drain(w_all.at[0, pl.ds(0, nz)], mate_sem.at[3])
    later(drain, w_all.at[0, pl.ds(0, nz)], mate_sem.at[2])

    def row_id(t):
        return tile_ref[0, t] % (2 * cols)

    def col_id(t):
        block = tile_ref[1, t]
        return block // (2 * cols) * 2 + block % 2

    def column_of(line):
        return jnp.sum(jnp.where(diagonal, line, 0.0), axis=1, keepdims=True)

    def reduce_tile(t, scores):
        top = jnp.max(scores, axis=0, keepdims=True)
        tile_top[pl.ds(t, 1), :] = top
        tile_sum[pl.ds(t, 1), :] = jnp.sum(jnp.exp2(scores - top), axis=0, keepdims=True)

    def product(left, right):
        return lax.dot_general(left, right, (((1,), (1,)), ((), ())), preferred_element_type=F32) * (4.0 * LOG2E)

    def loop(body, unroll):
        def step(t, carry):
            body(t)
            return carry

        lax.fori_loop(0, tiles, step, 0, unroll=unroll)

    def combine(id_of, blocks):
        alive = lax.broadcasted_iota(jnp.int32, (tiles, BLOCK), 0) < count_ref[0]
        tile_lse[...] = jnp.where(alive, tile_top[...] + jnp.log2(tile_sum[...]), NEGATIVE)
        place = lax.broadcasted_iota(jnp.int32, (blocks, BLOCK), 0)

        def top_of(t, top):
            return jnp.maximum(top, jnp.where(place == id_of(t), tile_lse[pl.ds(t, 1), :], NEGATIVE))

        top = lax.fori_loop(0, tiles, top_of, jnp.full((blocks, BLOCK), NEGATIVE, F32), unroll=4)
        block_top[pl.ds(0, blocks), :] = top

        def sum_of(t, total):
            home = id_of(t)
            share = jnp.exp2(tile_lse[pl.ds(t, 1), :] - block_top[pl.ds(home, 1), :])
            return total + jnp.where(place == home, share, 0.0)

        total = lax.fori_loop(0, tiles, sum_of, jnp.zeros((blocks, BLOCK), F32), unroll=4)
        return top + jnp.log2(jnp.maximum(total, TINY))

    def merge(parts):
        top = jnp.max(parts, axis=0)
        return top + jnp.log2(jnp.sum(jnp.exp2(parts - top[None]), axis=0))

    def spread(value, out):
        for k in range(value.shape[0] // 2):
            out[k] = value[2 * k : 2 * k + 2, :]

    def each(count, body):
        def step(k, carry):
            body(count // 2 + k // 2 * (1 - k % 2 * 2))
            return carry

        lax.fori_loop(1, count, step, 0)

    a_all[col] = log_a[...]

    def send_a(k):
        remote(log_a, a_all.at[col], u_sem.at[0, 0], u_sem.at[0, 1], (row, (col + k) % cols)).start()

    each(cols, send_a)
    later(drain, a_all.at[pl.ds(0, cols - 1)], u_sem.at[0, 0])

    for it in range(ITERS):
        def f_tile(t):
            line, part = col_id(t) // 2, col_id(t) % 2
            if it == 0:
                kt[t] = product(y_all[col_id(t)], x_all[row_id(t)])
            reduce_tile(t, kt[t] + column_of(w_all[it, line, pl.ds(part, 1), :]))

        loop(f_tile, UNROLL)
        f_send[it] = combine(row_id, cols * 2)

        def send_f(k):
            remote(
                f_send.at[it], f_recv.at[it, col], f_sem.at[it, 0], f_sem.at[it, 1], (row, (col + k) % cols)
            ).start()

        each(cols, send_f)
        later(drain, f_recv.at[it, pl.ds(0, cols - 1)], f_sem.at[it, 0])
        f_recv[it, col] = f_send[it]
        if it == 0:

            def other(t):
                kk[t] = product(x_all[row_id(t)], y_all[col_id(t)])

            loop(other, 4)
            drain(a_all.at[pl.ds(0, cols - 1)], u_sem.at[0, 1])
            for k in range(cols):
                a_rows[2 * k : 2 * k + 2, :] = a_all[k]
        drain(f_recv.at[it, pl.ds(0, cols - 1)], f_sem.at[it, 1])
        lse = merge(f_recv[it])
        u_all[...] = LOG2E * a_rows[...] - lse
        if it == ITERS - 1:
            block_top[pl.ds(0, cols * 2), :] = lse
            for part in range(2):
                own = block_top[pl.ds(2 * col + part, 1), :]
                f_out[part : part + 1, :] = 0.5 * x_square[part : part + 1, :] - (0.25 * LN2) * own

        def g_tile(t):
            reduce_tile(t, kk[t] + column_of(u_all[pl.ds(row_id(t), 1), :]))

        loop(g_tile, UNROLL)
        spread(combine(col_id, rows * 2), g_send.at[it])

        def send_g(k):
            owner = (row + k) % rows
            remote(
                g_send.at[it, owner], g_recv.at[it, row], g_sem.at[it, 0], g_sem.at[it, 1], (owner, col)
            ).start()

        each(rows, send_g)
        later(drain, g_recv.at[it, pl.ds(0, rows - 1)], g_sem.at[it, 0])
        g_recv[it, row] = g_send[it, row]
        drain(g_recv.at[it, pl.ds(0, rows - 1)], g_sem.at[it, 1])
        lse = merge(g_recv[it])
        if it == ITERS - 1:
            g_out[...] = 0.5 * y_square[...] - (0.25 * LN2) * lse
        else:
            w_all[it + 1, row] = LOG2E * log_b[...] - lse

            def send_w(k):
                line = w_all.at[it + 1, row]
                remote(line, line, w_sem.at[it, 0], w_sem.at[it, 1], ((row + k) % rows, col)).start()

            each(rows, send_w)
            later(drain, w_all.at[it + 1, pl.ds(0, rows - 1)], w_sem.at[it, 0])
            drain(w_all.at[it + 1, pl.ds(0, rows - 1)], w_sem.at[it, 1])

    for wait in pending:
        wait()


def body(dims, x_points, y_points, log_a, log_b, g_init, tile_list, tile_count):
    nz, nx, ny = dims
    rows, cols = nz * CORES, nx * ny
    width = x_points.shape[1]
    tiles = tile_list.shape[0]
    half = nz // 2
    vmem = pl.BlockSpec(memory_space=pltpu.VMEM)
    smem = pl.BlockSpec(memory_space=pltpu.SMEM)
    anywhere = pl.BlockSpec(memory_space=pl.ANY)
    dma = pltpu.SemaphoreType.DMA
    line = jax.ShapeDtypeStruct((2, BLOCK), F32)
    f_out, g_out = pl.pallas_call(
        functools.partial(kernel, dims),
        out_shape=(line, line),
        in_specs=[smem, smem, anywhere, anywhere, vmem, vmem, vmem],
        out_specs=(vmem, vmem),
        scratch_shapes=[
            pltpu.VMEM((cols * 2, BLOCK, width), jnp.bfloat16),
            pltpu.VMEM((rows * 2, BLOCK, width), jnp.bfloat16),
            pltpu.VMEM((ITERS, rows, 2, BLOCK), F32),
            pltpu.VMEM((cols * 2, BLOCK), F32),
            pltpu.VMEM((cols, 2, BLOCK), F32),
            pltpu.VMEM((cols * 2, BLOCK), F32),
            pltpu.VMEM((tiles, BLOCK, BLOCK), F32),
            pltpu.VMEM((tiles, BLOCK, BLOCK), F32),
            pltpu.VMEM((tiles, BLOCK), F32),
            pltpu.VMEM((tiles, BLOCK), F32),
            pltpu.VMEM((tiles, BLOCK), F32),
            pltpu.VMEM((max(rows, cols) * 2, BLOCK), F32),
            pltpu.VMEM((ITERS, cols * 2, BLOCK), F32),
            pltpu.VMEM((ITERS, cols, cols * 2, BLOCK), F32),
            pltpu.VMEM((ITERS, rows, 2, BLOCK), F32),
            pltpu.VMEM((ITERS, rows, 2, BLOCK), F32),
            pltpu.VMEM((2, BLOCK), F32),
            pltpu.VMEM((2, BLOCK), F32),
            dma((2,)),
            dma((2, half + 1, PIECES)),
            dma((2, half + 1, PIECES)),
            dma((2, half + 1)),
            dma((2, half + 1)),
            dma((4,)),
            dma((2, 2, 2, 2, 4)),
            dma((2, 2, 2, 2, 4)),
            dma((ITERS, 2)),
            dma((ITERS, 2)),
            dma((ITERS, 2)),
            dma((ITERS, 2)),
        ],
        compiler_params=pltpu.CompilerParams(collective_id=0, has_side_effects=True),
    )(
        tile_list.T,
        tile_count,
        x_points.reshape(2, BLOCK, width),
        y_points.reshape(2, BLOCK, width),
        log_a.reshape(2, BLOCK),
        log_b.reshape(2, BLOCK),
        g_init.reshape(2, BLOCK),
    )
    return f_out.reshape(-1), g_out.reshape(-1)


def solution(mesh):
    rows, cols = mesh.shape["row"], mesh.shape["col"]
    side = math.isqrt(cols)
    dims = (rows // CORES, cols // side, side)
    whole = P(("row", "col"))
    grid = P(("row", "col"), None)
    return jax.shard_map(
        functools.partial(body, dims),
        mesh=mesh,
        in_specs=(grid, grid, whole, whole, whole, grid, whole),
        out_specs=(whole, whole),
        check_vma=False,
    )
```

```python
import functools
import math

import jax
import jax.numpy as jnp
from jax import lax
from jax.experimental import pallas as pl
from jax.experimental.pallas import tpu as pltpu
from jax.sharding import PartitionSpec as P

MESH = pl.DeviceIdType.MESH
BLOCK = 128
ITERS = 2
CORES = 2
LOG2E = math.log2(math.e)
LN2 = math.log(2.0)
NEGATIVE = -1e30
TINY = 1e-37
F32 = jnp.float32
PIECES = 4
UNROLL = 24


def kernel(
    dims,
    tile_ref, count_ref, x_hbm, y_hbm, log_a, log_b, g_init,
    f_out, g_out,
    x_all, y_all, w_all, u_all, a_all, a_rows, kt, kk, tile_top, tile_sum, tile_lse, block_top,
    f_send, f_recv, g_send, g_recv, x_square, y_square,
    in_sem, ring_send, ring_recv, wring_send, wring_recv, mate_sem, xa_send, xa_recv,
    f_sem, u_sem, g_sem, w_sem,
):
    nz, nx, ny = dims
    rows, cols = nz * CORES, nx * ny
    tiles = tile_ref.shape[1]
    half = nz // 2
    row, col = lax.axis_index("row"), lax.axis_index("col")
    z, core = row // CORES, row % CORES
    px, py = col // ny, col % ny
    mate = (z * CORES + 1 - core, col)

    def at_z(step):
        return (z + step + nz) % nz * CORES + core

    def at_x(step):
        return (px + step) % nx * ny + py

    def at_y(step):
        return px * ny + (py + step) % ny

    def remote(src, dst, send, recv, device):
        return pltpu.make_async_remote_copy(
            src_ref=src, dst_ref=dst, send_sem=send, recv_sem=recv, device_id=device, device_id_type=MESH
        )

    def drain(ref, sem):
        pltpu.make_async_copy(ref, ref, sem).wait()

    pending = []

    def later(wait, *args):
        pending.append(lambda: wait(*args))

    load_x = pltpu.make_async_copy(x_hbm, x_all.at[pl.ds(2 * col, 2)], in_sem.at[0])
    load_y = pltpu.make_async_copy(y_hbm, y_all.at[pl.ds(2 * row, 2)], in_sem.at[1])
    load_y.start()
    load_x.start()

    barrier = pltpu.get_barrier_semaphore()
    greeted = [mate, (at_z(1), col), (at_z(-1), col)]
    greeted += [(row, at_x(1)), (row, at_x(nx - 1)), (row, at_y(1)), (row, at_y(ny - 1))]
    for device in greeted:
        pl.semaphore_signal(barrier, inc=1, device_id=device, device_id_type=MESH)
    pl.semaphore_wait(barrier, len(greeted))


    size = 2 * BLOCK // PIECES

    def piece(origin, part):
        return y_all.at[origin * 2 + part * size // BLOCK, pl.ds(part * size % BLOCK, size)]

    def ring(way, step, part):
        block = piece(at_z(-(step - 1) if way == 0 else step - 1), part)
        return remote(
            block, block, ring_send.at[way, step, part], ring_recv.at[way, step, part],
            (at_z(1 if way == 0 else -1), col),
        )

    def wring(way, step):
        origin = at_z(-(step - 1) if way == 0 else step - 1)
        line = w_all.at[0, origin]
        return remote(
            line, line, wring_send.at[way, step], wring_recv.at[way, step], (at_z(1 if way == 0 else -1), col)
        )

    def to_mate(origin, part):
        block = piece(origin, part)
        return remote(block, block, mate_sem.at[0], mate_sem.at[1], mate)

    def w_to_mate(origin):
        line = w_all.at[0, origin]
        return remote(line, line, mate_sem.at[2], mate_sem.at[3], mate)

    def go(copy):
        copy.start()
        later(copy.wait_send)

    def travels(way, step, part):
        return 1 <= step < half or (step == half and (part < PIECES // 2) == (way == 0))

    def at_line(axis, step):
        return at_x(step) if axis == 0 else at_y(step)

    def at_both(axis, one, two):
        x, y = (one, two) if axis == 0 else (two, one)
        return (px + x + nx) % nx * ny + (py + y + ny) % ny

    def plane(lane, phase, way, hop, index):
        axis = lane if phase == 0 else 1 - lane
        sign = 1 if way == 0 else -1
        back = 0 if hop == 0 else -sign
        origin = at_both(lane, back, 0) if phase == 0 else at_both(lane, index, back)
        block = x_all.at[2 * origin + lane]
        if hop == 1:
            block = block.at[pl.ds(way * (BLOCK // 2), BLOCK // 2)]
        sems = (lane, phase, way, hop, index)
        return remote(block, block, xa_send.at[sems], xa_recv.at[sems], (row, at_line(axis, sign)))

    load_y.wait()
    for part in range(PIECES):
        for way in range(2):
            if travels(way, 1, part):
                go(ring(way, 1, part))
    load_x.wait()
    for lane in range(2):
        for way in range(2):
            go(plane(lane, 0, way, 0, 0))
    for lane in range(2):
        for way in range(2):
            go(plane(lane, 1, way, 0, 0))
    for part in range(PIECES):
        to_mate(row, part).start()

    diagonal = lax.broadcasted_iota(jnp.int32, (BLOCK, BLOCK), 0) == lax.broadcasted_iota(
        jnp.int32, (BLOCK, BLOCK), 1
    )

    def squares(block):
        value = block.astype(F32)
        total = jnp.sum(value * value, axis=1, keepdims=True)
        return jnp.sum(jnp.where(diagonal, total, 0.0), axis=0, keepdims=True)

    for part in range(2):
        y_square[part : part + 1, :] = squares(y_all[2 * row + part])
    w_all[0, row] = LOG2E * (4.0 * g_init[...] - 2.0 * y_square[...] + log_b[...])
    go(wring(0, 1))
    if half > 1:
        go(wring(1, 1))
    w_to_mate(row).start()
    for part in range(2):
        x_square[part : part + 1, :] = squares(x_all[2 * col + part])

    def plane_steps(stage):
        for lane in range(2):
            if stage == 1:
                for way in range(2):
                    plane(lane, 0, way, 0, 0).wait_recv()
                    go(plane(lane, 0, way, 1, 0))
                    for out in range(2):
                        go(plane(lane, 1, out, 0, 3 if way == 0 else 1))
            if stage == 2:
                for way in range(2):
                    plane(lane, 0, way, 1, 0).wait_recv()
                for out in range(2):
                    go(plane(lane, 1, out, 0, 2))
            if stage in (1, 2, 3, 4):
                index = (0, 0, 1, 3, 2)[stage]
                for way in range(2):
                    plane(lane, 1, way, 0, index).wait_recv()
                    go(plane(lane, 1, way, 1, index))
            if stage == 5:
                for index in range(4):
                    for way in range(2):
                        plane(lane, 1, way, 1, index).wait_recv()

    def pass_lines(step):
        for way in range(2):
            if 1 <= step < half or (step == half and way == 0):
                wring(way, step).wait_recv()
                if step + 1 < half or (step + 1 == half and way == 0):
                    go(wring(way, step + 1))
                w_to_mate(at_z(-step if way == 0 else step)).start()

    for step in range(1, max(half, 5) + 1):
        for part in range(PIECES):
            for way in range(2):
                if not travels(way, step, part):
                    continue
                ring(way, step, part).wait_recv()
                if travels(way, step + 1, part):
                    go(ring(way, step + 1, part))
                to_mate(at_z(-step if way == 0 else step), part).start()
            if part == 0 and step <= half:
                pass_lines(step - 1)
        plane_steps(step)
    pass_lines(half)
    drain(y_all.at[pl.ds(0, rows)], mate_sem.at[1])
    later(drain, y_all.at[pl.ds(0, rows)], mate_sem.at[0])
    drain(w_all.at[0, pl.ds(0, nz)], mate_sem.at[3])
    later(drain, w_all.at[0, pl.ds(0, nz)], mate_sem.at[2])

    def row_id(t):
        return tile_ref[0, t] % (2 * cols)

    def col_id(t):
        block = tile_ref[1, t]
        return block // (2 * cols) * 2 + block % 2

    def column_of(line):
        return jnp.sum(jnp.where(diagonal, line, 0.0), axis=1, keepdims=True)

    def reduce_tile(t, scores):
        top = jnp.max(scores, axis=0, keepdims=True)
        tile_top[pl.ds(t, 1), :] = top
        tile_sum[pl.ds(t, 1), :] = jnp.sum(jnp.exp2(scores - top), axis=0, keepdims=True)

    def product(left, right):
        return lax.dot_general(left, right, (((1,), (1,)), ((), ())), preferred_element_type=F32) * (4.0 * LOG2E)

    def loop(body, unroll):
        def step(t, carry):
            body(t)
            return carry

        lax.fori_loop(0, tiles, step, 0, unroll=unroll)

    def combine(id_of, blocks):
        alive = lax.broadcasted_iota(jnp.int32, (tiles, BLOCK), 0) < count_ref[0]
        tile_lse[...] = jnp.where(alive, tile_top[...] + jnp.log2(tile_sum[...]), NEGATIVE)
        place = lax.broadcasted_iota(jnp.int32, (blocks, BLOCK), 0)

        def top_of(t, top):
            return jnp.maximum(top, jnp.where(place == id_of(t), tile_lse[pl.ds(t, 1), :], NEGATIVE))

        top = lax.fori_loop(0, tiles, top_of, jnp.full((blocks, BLOCK), NEGATIVE, F32), unroll=4)
        block_top[pl.ds(0, blocks), :] = top

        def sum_of(t, total):
            home = id_of(t)
            share = jnp.exp2(tile_lse[pl.ds(t, 1), :] - block_top[pl.ds(home, 1), :])
            return total + jnp.where(place == home, share, 0.0)

        total = lax.fori_loop(0, tiles, sum_of, jnp.zeros((blocks, BLOCK), F32), unroll=4)
        return top + jnp.log2(jnp.maximum(total, TINY))

    def merge(parts):
        top = jnp.max(parts, axis=0)
        return top + jnp.log2(jnp.sum(jnp.exp2(parts - top[None]), axis=0))

    def spread(value, out):
        for k in range(value.shape[0] // 2):
            out[k] = value[2 * k : 2 * k + 2, :]

    def each(count, body):
        def step(k, carry):
            body(count // 2 + k // 2 * (1 - k % 2 * 2))
            return carry

        lax.fori_loop(1, count, step, 0)

    a_all[col] = log_a[...]

    def send_a(k):
        remote(log_a, a_all.at[col], u_sem.at[0, 0], u_sem.at[0, 1], (row, (col + k) % cols)).start()

    each(cols, send_a)
    later(drain, a_all.at[pl.ds(0, cols - 1)], u_sem.at[0, 0])

    for it in range(ITERS):
        def f_tile(t):
            line, part = col_id(t) // 2, col_id(t) % 2
            if it == 0:
                kt[t] = product(y_all[col_id(t)], x_all[row_id(t)])
            reduce_tile(t, kt[t] + column_of(w_all[it, line, pl.ds(part, 1), :]))

        loop(f_tile, UNROLL)
        f_send[it] = combine(row_id, cols * 2)

        def send_f(k):
            remote(
                f_send.at[it], f_recv.at[it, col], f_sem.at[it, 0], f_sem.at[it, 1], (row, (col + k) % cols)
            ).start()

        each(cols, send_f)
        later(drain, f_recv.at[it, pl.ds(0, cols - 1)], f_sem.at[it, 0])
        f_recv[it, col] = f_send[it]
        if it == 0:

            def other(t):
                kk[t] = product(x_all[row_id(t)], y_all[col_id(t)])

            loop(other, 4)
            drain(a_all.at[pl.ds(0, cols - 1)], u_sem.at[0, 1])
            for k in range(cols):
                a_rows[2 * k : 2 * k + 2, :] = a_all[k]
        drain(f_recv.at[it, pl.ds(0, cols - 1)], f_sem.at[it, 1])
        lse = merge(f_recv[it])
        u_all[...] = LOG2E * a_rows[...] - lse
        if it == ITERS - 1:
            block_top[pl.ds(0, cols * 2), :] = lse
            for part in range(2):
                own = block_top[pl.ds(2 * col + part, 1), :]
                f_out[part : part + 1, :] = 0.5 * x_square[part : part + 1, :] - (0.25 * LN2) * own

        def g_tile(t):
            reduce_tile(t, kk[t] + column_of(u_all[pl.ds(row_id(t), 1), :]))

        loop(g_tile, UNROLL)
        spread(combine(col_id, rows * 2), g_send.at[it])

        def send_g(k):
            owner = (row + k) % rows
            remote(
                g_send.at[it, owner], g_recv.at[it, row], g_sem.at[it, 0], g_sem.at[it, 1], (owner, col)
            ).start()

        each(rows, send_g)
        later(drain, g_recv.at[it, pl.ds(0, rows - 1)], g_sem.at[it, 0])
        g_recv[it, row] = g_send[it, row]
        drain(g_recv.at[it, pl.ds(0, rows - 1)], g_sem.at[it, 1])
        lse = merge(g_recv[it])
        if it == ITERS - 1:
            g_out[...] = 0.5 * y_square[...] - (0.25 * LN2) * lse
        else:
            w_all[it + 1, row] = LOG2E * log_b[...] - lse

            def send_w(k):
                line = w_all.at[it + 1, row]
                remote(line, line, w_sem.at[it, 0], w_sem.at[it, 1], ((row + k) % rows, col)).start()

            each(rows, send_w)
            later(drain, w_all.at[it + 1, pl.ds(0, rows - 1)], w_sem.at[it, 0])
            drain(w_all.at[it + 1, pl.ds(0, rows - 1)], w_sem.at[it, 1])

    for wait in pending:
        wait()


def body(dims, x_points, y_points, log_a, log_b, g_init, tile_list, tile_count):
    nz, nx, ny = dims
    rows, cols = nz * CORES, nx * ny
    width = x_points.shape[1]
    tiles = tile_list.shape[0]
    half = nz // 2
    vmem = pl.BlockSpec(memory_space=pltpu.VMEM)
    smem = pl.BlockSpec(memory_space=pltpu.SMEM)
    anywhere = pl.BlockSpec(memory_space=pl.ANY)
    dma = pltpu.SemaphoreType.DMA
    line = jax.ShapeDtypeStruct((2, BLOCK), F32)
    f_out, g_out = pl.pallas_call(
        functools.partial(kernel, dims),
        out_shape=(line, line),
        in_specs=[smem, smem, anywhere, anywhere, vmem, vmem, vmem],
        out_specs=(vmem, vmem),
        scratch_shapes=[
            pltpu.VMEM((cols * 2, BLOCK, width), jnp.bfloat16),
            pltpu.VMEM((rows * 2, BLOCK, width), jnp.bfloat16),
            pltpu.VMEM((ITERS, rows, 2, BLOCK), F32),
            pltpu.VMEM((cols * 2, BLOCK), F32),
            pltpu.VMEM((cols, 2, BLOCK), F32),
            pltpu.VMEM((cols * 2, BLOCK), F32),
            pltpu.VMEM((tiles, BLOCK, BLOCK), F32),
            pltpu.VMEM((tiles, BLOCK, BLOCK), F32),
            pltpu.VMEM((tiles, BLOCK), F32),
            pltpu.VMEM((tiles, BLOCK), F32),
            pltpu.VMEM((tiles, BLOCK), F32),
            pltpu.VMEM((max(rows, cols) * 2, BLOCK), F32),
            pltpu.VMEM((ITERS, cols * 2, BLOCK), F32),
            pltpu.VMEM((ITERS, cols, cols * 2, BLOCK), F32),
            pltpu.VMEM((ITERS, rows, 2, BLOCK), F32),
            pltpu.VMEM((ITERS, rows, 2, BLOCK), F32),
            pltpu.VMEM((2, BLOCK), F32),
            pltpu.VMEM((2, BLOCK), F32),
            dma((2,)),
            dma((2, half + 1, PIECES)),
            dma((2, half + 1, PIECES)),
            dma((2, half + 1)),
            dma((2, half + 1)),
            dma((4,)),
            dma((2, 2, 2, 2, 4)),
            dma((2, 2, 2, 2, 4)),
            dma((ITERS, 2)),
            dma((ITERS, 2)),
            dma((ITERS, 2)),
            dma((ITERS, 2)),
        ],
        compiler_params=pltpu.CompilerParams(collective_id=0, has_side_effects=True),
    )(
        tile_list.T,
        tile_count,
        x_points.reshape(2, BLOCK, width),
        y_points.reshape(2, BLOCK, width),
        log_a.reshape(2, BLOCK),
        log_b.reshape(2, BLOCK),
        g_init.reshape(2, BLOCK),
    )
    return f_out.reshape(-1), g_out.reshape(-1)


def solution(mesh):
    rows, cols = mesh.shape["row"], mesh.shape["col"]
    side = math.isqrt(cols)
    dims = (rows // CORES, cols // side, side)
    whole = P(("row", "col"))
    grid = P(("row", "col"), None)
    return jax.shard_map(
        functools.partial(body, dims),
        mesh=mesh,
        in_specs=(grid, grid, whole, whole, whole, grid, whole),
        out_specs=(whole, whole),
        check_vma=False,
    )
```
